32 devices in a mesh: ctx: 16 (over z, y, x), dp: 2 (over core).
Axes of the slice: x: 2, y: 2, z: 4, core: 2. Of those that a mesh axis runs over, the one named last changes fastest.
Arguments:
- inputs: bfloat16 [2, 2048, 12288], P('dp', 'ctx'), may hold values from -6 to 6
- feat_weight: float32 [7, 12288], P(None, 'dp'), may hold values from -2 to 2
- filter_taps: float32 [128, 4096], P(None, 'dp'), may hold values from -0.5 to 0.5
- upstream: bfloat16 [2, 2048, 4096], P('dp', 'ctx'), may hold values from -6 to 6
Outputs:
- filter_grad: float32 [128, 4096], P(None, 'dp')
- feat_grad: float32 [7, 12288], P(None, 'dp')
The draws below stay inside these ranges and needn't reach their ends.
All inputs are finite; a program needn't handle non-finite values.
Results may differ from the reference program's by a relative error of at most 0.0041.
Values may be sent and summed in bfloat16 or wider, within the bound.
A program may use at most 128 MiB of HBM per device.

```python
import jax
import jax.numpy as jnp
from jax import lax

C = 4096
FEAT = 7
FILT = 128
TOKENS = 2048
SEQS = 2


def with_spikes(values, key, source, target, blocks, factor):
    def block_of(dim):
        return (jnp.arange(values.shape[dim]) // (values.shape[dim] // blocks)).reshape((-1,) + (1,) * (values.ndim - 1 - dim))

    first = jax.random.permutation(key, blocks)[block_of(target)]
    other_side = (block_of(target) + blocks // 2) % blocks
    return jnp.where((block_of(source) == first) | (block_of(source) == other_side), factor * values, values)


def levels(stream_key, dims, cuts, smallest, high):
    factor_of, own = 1.0, jax.random.fold_in(stream_key, 6)
    for dim, blocks in cuts:
        heights = jnp.exp(jax.random.uniform(jax.random.fold_in(own, dim), (blocks,), jnp.float32, smallest / len(cuts), high / len(cuts)))
        factor_of = factor_of * jnp.repeat(heights, dims[dim] // blocks).reshape([-1 if axis == dim else 1 for axis in range(len(dims))])
    return factor_of


def bell_draw(own_key, extent, spread, limit, pieces=(), kind=jnp.bfloat16):
    values = jax.random.normal(own_key, extent, jnp.float32) * spread
    if len(pieces) > 0:
        values = levels(own_key, extent, pieces, -0.22, 0.18) * values
    return jnp.clip(values, min=-limit, max=limit).astype(kind)


def noise_with(key, extent, width, most, split, heavy, kind=jnp.bfloat16):
    entries = width * jax.random.normal(key, extent, jnp.float32)
    if split:
        entries = entries * levels(key, extent, split, -0.22, 0.18)
    return jnp.clip(with_spikes(entries, jax.random.fold_in(key, 3), *heavy), -most, most).astype(kind)


def setup_inputs(seed: int = 0) -> dict:
    splits = jax.random.split(jax.random.key(seed), 5)
    inputs = bell_draw(splits[0], (SEQS, TOKENS, 3 * C), 1.0, 6.0, ((0, 2), (1, 16)))
    feat_weight = bell_draw(splits[1], (FEAT, 3 * C), FEAT ** -0.5, 2.0, ((1, 2),), jnp.float32)
    filter_taps = bell_draw(splits[2], (FILT, C), FILT ** -0.5, 0.5, ((1, 2),), jnp.float32)
    upstream = noise_with(splits[3], (SEQS, TOKENS, C), 1.0, 6.0, ((0, 2), (1, 16)), (0, 2, 2, 2.0))
    return dict(inputs=inputs, feat_weight=feat_weight, filter_taps=filter_taps, upstream=upstream)


def delayed(values, steps):
    if steps == 0:
        return values
    padding = jnp.zeros((steps,) + values.shape[1:], values.dtype)
    return jnp.concatenate([padding, values[:values.shape[0] - steps]], 0)


def sequence_terms(operands, feat_weight, filter_taps):
    signal, grad_out = operands
    signal_wide = signal.astype(jnp.float32)
    featured = sum(feat_weight[offset] * delayed(signal_wide, offset) for offset in range(FEAT))
    query = featured[:, :C]
    key_part = featured[:, C:2 * C]
    value_part = featured[:, 2 * C:]
    mixed = (key_part * value_part).astype(jnp.bfloat16)
    seq_length = signal.shape[0]
    padded = 2 * seq_length
    mixed_hat = jnp.fft.rfft(mixed.astype(jnp.float32), n=padded, axis=0)
    taps_hat = jnp.fft.rfft(filter_taps, n=padded, axis=0)
    conv_out = jnp.fft.irfft(mixed_hat * taps_hat, n=padded, axis=0)[:seq_length]
    grad_wide = grad_out.astype(jnp.float32)
    grad_conv = (grad_wide * query).astype(jnp.bfloat16)
    grad_hat = jnp.fft.rfft(grad_conv.astype(jnp.float32), n=padded, axis=0)
    grad_mixed = jnp.fft.irfft(grad_hat * jnp.conj(taps_hat), n=padded, axis=0)[:seq_length]
    filter_part = jnp.fft.irfft(grad_hat * jnp.conj(mixed_hat), n=padded, axis=0)[:FILT]
    grad_feat = jnp.concatenate([grad_wide * conv_out, grad_mixed * value_part, grad_mixed * key_part], 1)
    feat_part = jnp.stack([jnp.sum(grad_feat * delayed(signal_wide, offset), 0) for offset in range(FEAT)], 0)
    return filter_part, feat_part


def reference(inputs, feat_weight, filter_taps, upstream):
    parts = lax.map(lambda operands: sequence_terms(operands, feat_weight, filter_taps), (inputs, upstream))
    scale = (SEQS * TOKENS) ** -0.5
    return jnp.sum(parts[0], 0) * scale, jnp.sum(parts[1], 0) * scale
```

```python
import functools

import jax
import jax.numpy as jnp
import numpy as np
from jax import lax
from jax.experimental import pallas as pl
from jax.experimental.pallas import tpu as pltpu
from jax.sharding import PartitionSpec as P

PAD = 8
F32 = jnp.float32
BF16 = jnp.bfloat16


def from_behind(block, axis, distance):
    devices = range(lax.axis_size(axis))
    route = [(i - distance, i) for i in devices if i - distance in devices]
    return lax.ppermute(block, axis, route)


def two_parts(matrix):
    high = matrix.astype(BF16)
    low = (matrix - high.astype(np.float64)).astype(BF16)
    return high, low


def transforms(rows, taps):
    size = rows + taps
    half = size // 2
    angle = 2 * np.pi * np.outer(np.arange(half), np.arange(size)) / size
    cosines = np.cos(angle)
    sines = -np.sin(angle)
    sines[0] = np.cos(np.pi * np.arange(size))
    forward = np.concatenate([cosines, sines], 0)
    weight = np.full((size, 1), 2.0 / size)
    weight[0] = weight[half] = 1.0 / size
    backward = (forward * weight).T
    f_high, f_low = two_parts(forward)
    b_high, b_low = two_parts(backward)
    cat = lambda *parts: np.concatenate(parts, 1)
    return (
        cat(f_high[:, :rows], f_low[:, :rows]),
        cat(f_high[:, :taps], f_low[:, :taps], f_high[:, :taps]),
        cat(f_high, f_low),
        cat(b_high, b_low),
    )


def dot(a, b):
    return jnp.dot(a, b, preferred_element_type=F32)


def chunk_terms(q_ext, k_ext, v_ext, up_ext, taps, weights, mats, rows, reach):
    to_mixed, to_taps, to_grad, back = mats
    size = up_ext.shape[0]
    half = size // 2

    def featured(ext, w, out_rows):
        total = w[0:1] * ext[PAD : PAD + out_rows, :]
        for j in range(1, reach):
            total += w[j : j + 1] * ext[PAD - j : PAD - j + out_rows, :]
        return total

    def lagged(grad, ext, out_rows):
        sums = [
            jnp.sum(grad * ext[PAD - j : PAD - j + out_rows, :], 0, keepdims=True)
            for j in range(reach)
        ]
        sums += [jnp.zeros_like(sums[0])] * (PAD - reach)
        return jnp.concatenate(sums, 0)

    key_part = featured(k_ext, weights[1], rows)
    value_part = featured(v_ext, weights[2], rows)
    mixed = (key_part * value_part).astype(BF16)
    m_hat = dot(to_mixed[...], jnp.concatenate([mixed, mixed], 0))
    taps_high = taps.astype(BF16)
    taps_low = (taps - taps_high.astype(F32)).astype(BF16)
    t_hat = dot(to_taps[...], jnp.concatenate([taps_high, taps_high, taps_low], 0))
    query = featured(q_ext, weights[0], size)
    grad_conv = (up_ext[...].astype(F32) * query).astype(BF16)
    g_hat = dot(to_grad[...], jnp.concatenate([grad_conv, grad_conv], 0))

    m_re, m_im = m_hat[:half], m_hat[half:]
    t_re, t_im = t_hat[:half], t_hat[half:]
    g_re, g_im = g_hat[:half], g_hat[half:]
    first = lax.broadcasted_iota(jnp.int32, m_re.shape, 0) == 0
    t_imz = jnp.where(first, 0.0, t_im)
    t_ren = jnp.where(first, t_im, t_re)
    m_imz = jnp.where(first, 0.0, m_im)
    m_ren = jnp.where(first, m_im, m_re)

    def inverse(re, im, out_rows):
        re, im = re.astype(BF16), im.astype(BF16)
        return dot(back[:out_rows, :], jnp.concatenate([re, im, re, im], 0))

    conv_out = inverse(
        m_re * t_re - m_im * t_imz, m_re * t_imz + m_im * t_ren, size
    )
    grad_mixed = inverse(
        g_re * t_re + g_im * t_imz, g_im * t_ren - g_re * t_imz, rows
    )
    filter_part = inverse(
        g_re * m_re + g_im * m_imz, g_im * m_ren - g_re * m_imz, taps.shape[0]
    )
    return (
        filter_part,
        lagged(up_ext[...].astype(F32) * conv_out, q_ext, size),
        lagged(grad_mixed * value_part, k_ext, rows),
        lagged(grad_mixed * key_part, v_ext, rows),
    )


def local_kernel(
    reach, xq, xk, xv, pq, pk, pv, nq, up, nup, taps, wq, wk, wv, m0, m1, m2, m3,
    filt, fq, fk, fv, q_ext, k_ext, v_ext, up_ext,
):
    rows = xq.shape[0]
    size = up_ext.shape[0]
    for ext, prev, block in ((q_ext, pq, xq), (k_ext, pk, xk), (v_ext, pv, xv)):
        ext[0:PAD, :] = prev[...].astype(F32)
        ext[PAD : PAD + rows, :] = block[...].astype(F32)
    q_ext[PAD + rows : PAD + size, :] = nq[...].astype(F32)
    up_ext[0:rows, :] = up[...]
    up_ext[rows:size, :] = nup[...]
    filt[...], fq[...], fk[...], fv[...] = chunk_terms(
        q_ext, k_ext, v_ext, up_ext, taps[...], (wq[...], wk[...], wv[...]),
        (m0, m1, m2, m3), rows, reach,
    )


def by_collectives(inputs, feat_weight, filter_taps, upstream):
    inputs_here = inputs[0]
    grad_here = upstream[0]
    rows = inputs_here.shape[0]
    channels = grad_here.shape[1]
    filt_rows = filter_taps.shape[0]
    reach = feat_weight.shape[0]
    scale = (lax.axis_size("dp") * lax.axis_size("ctx") * rows) ** (-0.5)
    feat_full, taps_full = (
        lax.all_gather(feat_weight, "dp", axis=1, tiled=True),
        lax.all_gather(filter_taps, "dp", axis=1, tiled=True),
    )
    next_grad, next_query = from_behind(
        (grad_here[:filt_rows], inputs_here[:filt_rows, :channels]), "ctx", -1
    )
    before = from_behind(inputs_here[rows - PAD :], "ctx", 1)
    weights = jnp.concatenate(
        [feat_full, jnp.zeros((PAD - reach, feat_full.shape[1]), F32)], 0
    )
    mats = [jnp.asarray(m) for m in transforms(rows, filt_rows)]
    width = 256
    steps = channels // width
    size = rows + filt_rows
    part = lambda r, group: pl.BlockSpec((r, width), lambda i: (0, i + group * steps))
    whole = lambda m: pl.BlockSpec(m.shape, lambda i: (0, 0))
    out = lambda r: jax.ShapeDtypeStruct((r, channels), F32)
    filter_part, feat_q, feat_k, feat_v = pl.pallas_call(
        functools.partial(local_kernel, reach),
        grid=(steps,),
        out_shape=[out(filt_rows), out(PAD), out(PAD), out(PAD)],
        in_specs=[part(rows, g) for g in range(3)]
        + [part(PAD, g) for g in range(3)]
        + [part(filt_rows, 0), part(rows, 0), part(filt_rows, 0), part(filt_rows, 0)]
        + [part(PAD, g) for g in range(3)]
        + [whole(m) for m in mats],
        out_specs=[part(filt_rows, 0)] + [part(PAD, 0)] * 3,
        scratch_shapes=[
            pltpu.VMEM((PAD + size, width), F32),
            pltpu.VMEM((PAD + rows, width), F32),
            pltpu.VMEM((PAD + rows, width), F32),
            pltpu.VMEM((size, width), BF16),
        ],
    )(
        inputs_here, inputs_here, inputs_here, before, before, before, next_query,
        grad_here, next_grad, taps_full, weights, weights, weights, *mats,
    )
    feat_part = jnp.concatenate([feat_q, feat_k, feat_v], 1)[:reach]
    filter_summed, feat_summed = (
        lax.psum_scatter(filter_part, "dp", scatter_dimension=1, tiled=True),
        lax.psum_scatter(feat_part, "dp", scatter_dimension=1, tiled=True),
    )
    filter_whole, feat_whole = lax.psum((filter_summed, feat_summed), "ctx")
    return (filter_whole * scale, feat_whole * scale)


MESH = pl.DeviceIdType.MESH
LANES = 128
PLANE = 4
TAIL = 16
AHEAD = 2


def fused_kernel(
    reach, x, up, taps_here, w_here, f0, f1, f2, f3, out,
    data, nxt, prev, taps_all, w_all, m0, m1, m2, m3, q_ext, k_ext, v_ext, up_ext,
    stage, dp_got, z_part, z_got, y_part, y_got, done, e_got,
    own_sem, fixed_sem, out_sem, swap_ssem, swap_rsem, x_ssem, x_rsem,
    nxt_ssem, nxt_rsem, tail_ssem, tail_rsem, dp_ssem, dp_rsem, z_ssem, z_rsem,
    y_ssem, y_rsem, e_ssem, e_rsem, ag_ssem, ag_rsem,
):
    n = lax.axis_size("ctx")
    me, core = lax.axis_index("ctx"), lax.axis_index("dp")
    side = lax.rem(me, 2)
    rows, channels = up.shape
    half = channels // 2
    filt_rows = taps_here.shape[0]
    chunks, planes = data.shape[1], z_got.shape[1]
    size = rows + filt_rows
    packed = stage.shape[2]
    level = me // PLANE
    partner = {"dp": 1 - core}
    across = {"ctx": me + 1 - 2 * side}
    beside = {"ctx": me + 2 - 4 * (lax.rem(me, PLANE) // 2)}
    before, after = {"ctx": lax.rem(me + n - 2, n)}, {"ctx": lax.rem(me + 2, n)}
    has_before, has_after = me >= 2, me < n - 2

    def column(k):
        return {"ctx": lax.rem(me + k * PLANE, n)}

    def plane_at(k):
        return lax.rem(level + k, planes)

    barrier = pltpu.get_barrier_semaphore()
    peers = [partner, across, before, after] + [column(k) for k in range(1, planes)]
    for peer in peers:
        pl.semaphore_signal(barrier, inc=1, device_id=peer, device_id_type=MESH)

    def local(src, dst, sem):
        return pltpu.make_async_copy(src, dst, sem)

    def remote(src, dst, send, got, device):
        return pltpu.make_async_remote_copy(
            src_ref=src, dst_ref=dst, send_sem=send, recv_sem=got,
            device_id=device, device_id_type=MESH,
        )

    def source(g, owner, c, p):
        low = (owner * chunks + c) * LANES + p * half + max(g - 1, 0) * channels
        at = pl.ds(pl.multiple_of(low, LANES), LANES)
        return x.at[:, at] if g else up.at[:, at]

    def place(owner, c, g, p):
        return data.at[owner, c, g, :, pl.ds(p * LANES, LANES)]

    def own_start(c):
        for g in range(4):
            for p in range(2):
                local(source(g, side, c, p), place(side, c, g, p), own_sem.at[c]).start()

    def own_wait(c):
        local(data.at[1 - side, c], data.at[side, c], own_sem.at[c]).wait()

    def x_start(c):
        for g in range(4):
            for p in range(2):
                remote(
                    source(g, 1 - side, c, p), place(side, c, g, p),
                    x_ssem.at[c, g // 2], x_rsem.at[c, g // 2], across,
                ).start()

    def x_whole(c, part):
        block = data.at[1 - side, c, pl.ds(2 * part, 2)]
        return remote(block, block, x_ssem.at[c, part], x_rsem.at[c, part], across)

    def nxt_copy(c):
        return remote(
            data.at[0, c, pl.ds(0, 2)], nxt.at[c], nxt_ssem.at[c], nxt_rsem.at[c], before
        )

    def tail_copy(c):
        return remote(
            data.at[1, c, pl.ds(1, 3), pl.ds(rows - TAIL, TAIL)], prev.at[c],
            tail_ssem.at[c], tail_rsem.at[c], after,
        )

    def dp_copy(c):
        return remote(
            stage.at[c, 1 - core], dp_got.at[c], dp_ssem.at[c], dp_rsem.at[c], partner
        )

    def z_copy(c, k):
        return remote(
            z_part.at[c, plane_at(k)], z_got.at[c, level], z_ssem.at[c, k],
            z_rsem.at[c, level], column(k),
        )

    def z_arrival(c, k):
        return remote(
            z_part.at[c, 0], z_got.at[c, plane_at(k)], z_ssem.at[c, k],
            z_rsem.at[c, plane_at(k)], column(k),
        )

    def y_copy(c):
        return remote(y_part.at[c], y_got.at[c], y_ssem.at[c], y_rsem.at[c], beside)

    def e_copy(c):
        return remote(done.at[c], e_got.at[c], e_ssem.at[c], e_rsem.at[c], across)

    def ag_copy(c, foreign, k):
        owner = (side + foreign - 2 * side * foreign) * chunks + c
        return remote(
            (e_got if foreign else done).at[c], out.at[owner, level],
            ag_ssem.at[c, foreign, k], ag_rsem.at[owner, level], column(k),
        )

    def ag_arrival(owner, k):
        return remote(
            done.at[0], out.at[owner, plane_at(k)], ag_ssem.at[0, 0, k],
            ag_rsem.at[owner, plane_at(k)], column(k),
        )

    def out_copy(c, foreign):
        owner = (side + foreign - 2 * side * foreign) * chunks + c
        return local(
            (e_got if foreign else done).at[c], out.at[owner, level], out_sem.at[c, foreign]
        )

    taps_side = pl.ds(pl.multiple_of(side * chunks * LANES, LANES), chunks * LANES)
    swaps = (
        remote(taps_here.at[:, taps_side], taps_all.at[core], swap_ssem.at[0], swap_rsem.at[0], partner),
        remote(w_here, w_all.at[core], swap_ssem.at[1], swap_rsem.at[1], partner),
    )
    kept = [
        local(taps_here.at[:, taps_side], taps_all.at[core], fixed_sem.at[0]),
        local(w_here, w_all.at[core], fixed_sem.at[1]),
    ] + [local(f, m, fixed_sem.at[2 + i]) for i, (f, m) in enumerate(((f0, m0), (f1, m1), (f2, m2), (f3, m3)))]

    own_start(0)
    for copy in kept:
        copy.start()

    @pl.loop(1, chunks)
    def _(c):
        own_start(c)

    pl.semaphore_wait(barrier, len(peers))

    @pl.loop(0, AHEAD)
    def _(c):
        x_start(c)

    for copy in swaps:
        copy.start()

    @pl.when(me < 2)
    def _():
        prev[...] = jnp.zeros_like(prev)

    @pl.when(me >= n - 2)
    def _():
        nxt[...] = jnp.zeros_like(nxt)

    for copy in kept:
        copy.wait()
    own_wait(0)

    @pl.when((side == 0) & has_before)
    def _():
        nxt_copy(0).start()

    @pl.when((side == 1) & has_after)
    def _():
        tail_copy(0).start()

    for copy in swaps:
        copy.wait()

    def block_terms(c, b, taps, weights):
        old = prev[c].astype(F32) if b == 0 else data[0, c, 1:4, rows - TAIL :, :].astype(F32)
        for g, ext in enumerate((q_ext, k_ext, v_ext)):
            ext[0:PAD, :] = old[g, TAIL - PAD :]
            ext[PAD : PAD + rows, :] = data[b, c, g + 1].astype(F32)
        ahead = (data[1, c, 0], data[1, c, 1]) if b == 0 else (nxt[c, 0], nxt[c, 1])
        q_ext[PAD + rows : PAD + size, :] = ahead[1].astype(F32)
        up_ext[0:rows, :] = data[b, c, 0]
        up_ext[rows:size, :] = ahead[0]
        return chunk_terms(
            q_ext, k_ext, v_ext, up_ext, taps, weights, (m0, m1, m2, m3), rows, reach
        )

    def compute(c):
        @pl.when(c + AHEAD < chunks)
        def _():
            x_start(c + AHEAD)

        @pl.when(c + 1 < chunks)
        def _():
            own_wait(c + 1)

        @pl.when((side == 0) & has_before & (c + 1 < chunks))
        def _():
            nxt_copy(c + 1).start()

        @pl.when((side == 1) & has_after & (c + 1 < chunks))
        def _():
            tail_copy(c + 1).start()

        x_whole(c, 0).wait_recv()

        @pl.when((side == 1) & has_before)
        def _():
            nxt_copy(c).start()

        x_whole(c, 1).wait_recv()

        @pl.when((side == 0) & has_after)
        def _():
            tail_copy(c).start()

        @pl.when(has_before)
        def _():
            tail_copy(c).wait_recv()

        here = pl.ds(pl.multiple_of(c * LANES, LANES), LANES)
        taps = jnp.concatenate([taps_all[p, :, here] for p in range(2)], 1)

        def weight(g, p):
            part, slot = divmod(2 * g + p, 3)
            low = (side * chunks + c) * LANES + slot * half
            return w_all[part, :, pl.ds(pl.multiple_of(low, LANES), LANES)]

        weights = [jnp.concatenate([weight(g, p) for p in range(2)], 1) for g in range(3)]
        first = block_terms(c, 0, taps, weights)

        @pl.when(has_after)
        def _():
            nxt_copy(c).wait_recv()

        second = block_terms(c, 1, taps, weights)
        filt, feat_q, feat_k, feat_v = [a + b for a, b in zip(first, second)]
        a, b = slice(0, LANES), slice(LANES, 2 * LANES)
        rest = [jnp.zeros((packed - filt_rows - 3 * PAD, LANES), F32)]
        stage[c, 0] = jnp.concatenate(
            [filt[:, a], feat_q[:, a], feat_q[:, b], feat_k[:, a]] + rest, 0
        )
        stage[c, 1] = jnp.concatenate(
            [filt[:, b], feat_k[:, b], feat_v[:, a], feat_v[:, b]] + rest, 0
        )
        dp_copy(c).start()

    def along_z(c):
        dp_copy(c).wait_recv()
        pair = stage[c, core] + dp_got[c]
        z_part[c] = pair.reshape(planes, packed // planes, LANES)
        for k in range(1, planes):
            z_copy(c, k).start()

    def along_y(c):
        total = z_part[c, level]
        for k in range(1, planes):
            z_arrival(c, k).wait_recv()
            total += z_got[c, plane_at(k)]
        y_part[c] = total
        y_copy(c).start()

    def share(c, foreign):
        for k in range(1, planes):
            ag_copy(c, foreign, k).start()
        out_copy(c, foreign).start()

    def along_x(c):
        y_copy(c).wait_recv()
        done[c] = (y_part[c] + y_got[c]).astype(BF16)
        e_copy(c).start()
        share(c, 0)

    def finish(c):
        e_copy(c).wait_recv()
        share(c, 1)

    steps = ((compute, 0), (along_z, 1), (along_y, 2), (along_x, 3), (finish, 5))

    @pl.loop(0, chunks + steps[-1][1])
    def _(i):
        for step, lag in steps:
            @pl.when((i >= lag) & (i - lag < chunks))
            def _():
                step(i - lag)

    @pl.loop(0, chunks)
    def _(c):
        for k in range(1, planes):
            ag_arrival(c, k).wait_recv()
            ag_arrival(c + chunks, k).wait_recv()
        for foreign in range(2):
            out_copy(c, foreign).wait()
            for k in range(1, planes):
                ag_copy(c, foreign, k).wait_send()
        for part in range(2):
            x_whole(c, part).wait_send()
        dp_copy(c).wait_send()
        for k in range(1, planes):
            z_copy(c, k).wait_send()
        y_copy(c).wait_send()
        e_copy(c).wait_send()

    @pl.when(has_before)
    def _():
        @pl.loop(0, chunks)
        def _(c):
            nxt_copy(c).wait_send()

    @pl.when(has_after)
    def _():
        @pl.loop(0, chunks)
        def _(c):
            tail_copy(c).wait_send()


def unpack_kernel(scale, reach, got, filt, feat):
    filt_rows = filt.shape[0]
    half = got.shape[0] * LANES
    for owner in range(got.shape[0]):
        value = got[owner].astype(F32).reshape(-1, LANES) * scale
        filt[:, owner * LANES : (owner + 1) * LANES] = value[:filt_rows]
        for g in range(3):
            low = filt_rows + g * PAD
            at = owner * LANES + g * half
            feat[:, at : at + LANES] = value[low : low + reach]


def fused(inputs, feat_weight, filter_taps, upstream):
    x, up = inputs[0], upstream[0]
    n = lax.axis_size("ctx")
    rows, channels = up.shape
    filt_rows, reach = filter_taps.shape[0], feat_weight.shape[0]
    scale = (lax.axis_size("dp") * n * rows) ** (-0.5)
    mats = [jnp.asarray(m) for m in transforms(rows, filt_rows)]
    size = rows + filt_rows
    width = 2 * LANES
    chunks = channels // (2 * width)
    planes = n // PLANE
    packed = -(-(filt_rows + 3 * PAD) // (planes * PAD)) * (planes * PAD)
    cut = packed // planes
    dma = lambda *shape: pltpu.SemaphoreType.DMA(shape)
    anywhere = pl.BlockSpec(memory_space=pl.ANY)
    gathered = pl.pallas_call(
        functools.partial(fused_kernel, reach),
        out_shape=jax.ShapeDtypeStruct((2 * chunks, planes, cut, LANES), BF16),
        in_specs=[anywhere] * 8,
        out_specs=anywhere,
        scratch_shapes=[
            pltpu.VMEM((2, chunks, 4, rows, width), BF16),
            pltpu.VMEM((chunks, 2, rows, width), BF16),
            pltpu.VMEM((chunks, 3, TAIL, width), BF16),
            pltpu.VMEM((2, filt_rows, chunks * LANES), F32),
            pltpu.VMEM((2,) + feat_weight.shape, F32),
            *[pltpu.VMEM(m.shape, BF16) for m in mats],
            pltpu.VMEM((PAD + size, width), F32),
            pltpu.VMEM((PAD + rows, width), F32),
            pltpu.VMEM((PAD + rows, width), F32),
            pltpu.VMEM((size, width), BF16),
            pltpu.VMEM((chunks, 2, packed, LANES), F32),
            pltpu.VMEM((chunks, packed, LANES), F32),
            pltpu.VMEM((chunks, planes, cut, LANES), F32),
            pltpu.VMEM((chunks, planes, cut, LANES), F32),
            pltpu.VMEM((chunks, cut, LANES), F32),
            pltpu.VMEM((chunks, cut, LANES), F32),
            pltpu.VMEM((chunks, cut, LANES), BF16),
            pltpu.VMEM((chunks, cut, LANES), BF16),
            dma(chunks), dma(6), dma(chunks, 2), dma(2), dma(2),
            dma(chunks, 2), dma(chunks, 2),
            *[dma(chunks)] * 6,
            dma(chunks, planes), dma(chunks, planes),
            *[dma(chunks)] * 4,
            dma(chunks, 2, planes), dma(2 * chunks, planes),
        ],
        compiler_params=pltpu.CompilerParams(
            collective_id=0, has_side_effects=True, vmem_limit_bytes=63 * 2**20
        ),
    )(x, up, filter_taps, feat_weight, *mats)
    return pl.pallas_call(
        functools.partial(unpack_kernel, scale, reach),
        out_shape=[
            jax.ShapeDtypeStruct(filter_taps.shape, F32),
            jax.ShapeDtypeStruct(feat_weight.shape, F32),
        ],
        in_specs=[pl.BlockSpec(memory_space=pltpu.VMEM)],
        out_specs=[pl.BlockSpec(memory_space=pltpu.VMEM)] * 2,
    )(gathered)


def per_device(inputs, feat_weight, filter_taps, upstream):
    n = lax.axis_size("ctx")
    rows, channels = upstream.shape[1:]
    whole = n % PLANE == 0 and n // PLANE > 1 and channels == 2 * n * LANES
    square = rows == filter_taps.shape[0] and feat_weight.shape[0] <= PAD
    if lax.axis_size("dp") == 2 and whole and square and rows % TAIL == 0:
        return fused(inputs, feat_weight, filter_taps, upstream)
    return by_collectives(inputs, feat_weight, filter_taps, upstream)


def solution(mesh):
    placed = (P("dp", "ctx", None), P(None, "dp"), P(None, "dp"), P("dp", "ctx", None))
    return jax.shard_map(
        per_device,
        mesh=mesh,
        in_specs=placed,
        out_specs=(P(None, "dp"), P(None, "dp")),
        check_vma=False,
    )
```

```python
import functools

import jax
import jax.numpy as jnp
import numpy as np
from jax import lax
from jax.experimental import pallas as pl
from jax.experimental.pallas import tpu as pltpu
from jax.sharding import PartitionSpec as P

PAD = 8
F32 = jnp.float32
BF16 = jnp.bfloat16


def from_behind(block, axis, distance):
    devices = range(lax.axis_size(axis))
    route = [(i - distance, i) for i in devices if i - distance in devices]
    return lax.ppermute(block, axis, route)


def two_parts(matrix):
    high = matrix.astype(BF16)
    low = (matrix - high.astype(np.float64)).astype(BF16)
    return high, low


def transforms(rows, taps):
    size = rows + taps
    half = size // 2
    angle = 2 * np.pi * np.outer(np.arange(half), np.arange(size)) / size
    cosines = np.cos(angle)
    sines = -np.sin(angle)
    sines[0] = np.cos(np.pi * np.arange(size))
    forward = np.concatenate([cosines, sines], 0)
    weight = np.full((size, 1), 2.0 / size)
    weight[0] = weight[half] = 1.0 / size
    backward = (forward * weight).T
    f_high, f_low = two_parts(forward)
    b_high, b_low = two_parts(backward)
    cat = lambda *parts: np.concatenate(parts, 1)
    return (
        cat(f_high[:, :rows], f_low[:, :rows]),
        cat(f_high[:, :taps], f_low[:, :taps], f_high[:, :taps]),
        cat(f_high, f_low),
        cat(b_high, b_low),
    )


def dot(a, b):
    return jnp.dot(a, b, preferred_element_type=F32)


def taps_transform(taps, to_taps):
    taps_high = taps.astype(BF16)
    taps_low = (taps - taps_high.astype(F32)).astype(BF16)
    return dot(to_taps[...], jnp.concatenate([taps_high, taps_high, taps_low], 0))


def inverse(re, im, back, out_rows):
    re, im = re.astype(BF16), im.astype(BF16)
    return dot(back[:out_rows, :], jnp.concatenate([re, im, re, im], 0))


def chunk_terms(q_ext, k_ext, v_ext, up_ext, t_hat, weights, mats, rows, reach):
    to_mixed, to_grad, back = mats
    size = up_ext.shape[0]
    half = size // 2

    def featured(ext, w, out_rows):
        total = w[0:1] * ext[PAD : PAD + out_rows, :]
        for j in range(1, reach):
            total += w[j : j + 1] * ext[PAD - j : PAD - j + out_rows, :]
        return total

    def lagged(grad, ext, out_rows):
        sums = [
            jnp.sum(grad * ext[PAD - j : PAD - j + out_rows, :], 0, keepdims=True)
            for j in range(reach)
        ]
        sums += [jnp.zeros_like(sums[0])] * (PAD - reach)
        return jnp.concatenate(sums, 0)

    key_part = featured(k_ext, weights[1], rows)
    value_part = featured(v_ext, weights[2], rows)
    mixed = (key_part * value_part).astype(BF16)
    m_hat = dot(to_mixed[...], jnp.concatenate([mixed, mixed], 0))
    query = featured(q_ext, weights[0], size)
    grad_conv = (up_ext[...].astype(F32) * query).astype(BF16)
    g_hat = dot(to_grad[...], jnp.concatenate([grad_conv, grad_conv], 0))

    m_re, m_im = m_hat[:half], m_hat[half:]
    t_re, t_im = t_hat[:half], t_hat[half:]
    g_re, g_im = g_hat[:half], g_hat[half:]
    first = lax.broadcasted_iota(jnp.int32, m_re.shape, 0) == 0
    t_imz = jnp.where(first, 0.0, t_im)
    t_ren = jnp.where(first, t_im, t_re)
    m_imz = jnp.where(first, 0.0, m_im)
    m_ren = jnp.where(first, m_im, m_re)

    conv_out = inverse(
        m_re * t_re - m_im * t_imz, m_re * t_imz + m_im * t_ren, back, size
    )
    grad_mixed = inverse(
        g_re * t_re + g_im * t_imz, g_im * t_ren - g_re * t_imz, back, rows
    )
    return (
        g_re * m_re + g_im * m_imz,
        g_im * m_ren - g_re * m_imz,
        lagged(up_ext[...].astype(F32) * conv_out, q_ext, size),
        lagged(grad_mixed * value_part, k_ext, rows),
        lagged(grad_mixed * key_part, v_ext, rows),
    )


def local_kernel(
    reach, xq, xk, xv, pq, pk, pv, nq, up, nup, taps, wq, wk, wv, m0, m1, m2, m3,
    filt, fq, fk, fv, q_ext, k_ext, v_ext, up_ext,
):
    rows = xq.shape[0]
    size = up_ext.shape[0]
    for ext, prev, block in ((q_ext, pq, xq), (k_ext, pk, xk), (v_ext, pv, xv)):
        ext[0:PAD, :] = prev[...].astype(F32)
        ext[PAD : PAD + rows, :] = block[...].astype(F32)
    q_ext[PAD + rows : PAD + size, :] = nq[...].astype(F32)
    up_ext[0:rows, :] = up[...]
    up_ext[rows:size, :] = nup[...]
    t_hat = taps_transform(taps[...], m1)
    cross_re, cross_im, fq[...], fk[...], fv[...] = chunk_terms(
        q_ext, k_ext, v_ext, up_ext, t_hat, (wq[...], wk[...], wv[...]),
        (m0, m2, m3), rows, reach,
    )
    filt[...] = inverse(cross_re, cross_im, m3, taps.shape[0])


def by_collectives(inputs, feat_weight, filter_taps, upstream):
    inputs_here = inputs[0]
    grad_here = upstream[0]
    rows = inputs_here.shape[0]
    channels = grad_here.shape[1]
    filt_rows = filter_taps.shape[0]
    reach = feat_weight.shape[0]
    scale = (lax.axis_size("dp") * lax.axis_size("ctx") * rows) ** (-0.5)
    feat_full, taps_full = (
        lax.all_gather(feat_weight, "dp", axis=1, tiled=True),
        lax.all_gather(filter_taps, "dp", axis=1, tiled=True),
    )
    next_grad, next_query = from_behind(
        (grad_here[:filt_rows], inputs_here[:filt_rows, :channels]), "ctx", -1
    )
    before = from_behind(inputs_here[rows - PAD :], "ctx", 1)
    weights = jnp.concatenate(
        [feat_full, jnp.zeros((PAD - reach, feat_full.shape[1]), F32)], 0
    )
    mats = [jnp.asarray(m) for m in transforms(rows, filt_rows)]
    width = 256
    steps = channels // width
    size = rows + filt_rows
    part = lambda r, group: pl.BlockSpec((r, width), lambda i: (0, i + group * steps))
    whole = lambda m: pl.BlockSpec(m.shape, lambda i: (0, 0))
    out = lambda r: jax.ShapeDtypeStruct((r, channels), F32)
    filter_part, feat_q, feat_k, feat_v = pl.pallas_call(
        functools.partial(local_kernel, reach),
        grid=(steps,),
        out_shape=[out(filt_rows), out(PAD), out(PAD), out(PAD)],
        in_specs=[part(rows, g) for g in range(3)]
        + [part(PAD, g) for g in range(3)]
        + [part(filt_rows, 0), part(rows, 0), part(filt_rows, 0), part(filt_rows, 0)]
        + [part(PAD, g) for g in range(3)]
        + [whole(m) for m in mats],
        out_specs=[part(filt_rows, 0)] + [part(PAD, 0)] * 3,
        scratch_shapes=[
            pltpu.VMEM((PAD + size, width), F32),
            pltpu.VMEM((PAD + rows, width), F32),
            pltpu.VMEM((PAD + rows, width), F32),
            pltpu.VMEM((size, width), BF16),
        ],
    )(
        inputs_here, inputs_here, inputs_here, before, before, before, next_query,
        grad_here, next_grad, taps_full, weights, weights, weights, *mats,
    )
    feat_part = jnp.concatenate([feat_q, feat_k, feat_v], 1)[:reach]
    filter_summed, feat_summed = (
        lax.psum_scatter(filter_part, "dp", scatter_dimension=1, tiled=True),
        lax.psum_scatter(feat_part, "dp", scatter_dimension=1, tiled=True),
    )
    filter_whole, feat_whole = lax.psum((filter_summed, feat_summed), "ctx")
    return (filter_whole * scale, feat_whole * scale)


MESH = pl.DeviceIdType.MESH
LANES = 128
PLANE = 4
TAIL = 16
AHEAD = 2


def fused_kernel(
    reach, x, up, taps_here, w_here, f0, f1, f2, f3, out,
    data, prev, taps_all, w_all, m0, m1, m2, m3, q_ext, k_ext, v_ext, up_ext,
    stage, dp_got, z_part, z_got, y_part, y_got, done, e_got,
    own_sem, fixed_sem, out_sem, swap_ssem, swap_rsem, x_ssem, x_rsem,
    nxt_ssem, nxt_rsem, tail_ssem, tail_rsem, dp_ssem, dp_rsem, z_ssem, z_rsem,
    y_ssem, y_rsem, e_ssem, e_rsem, ag_ssem, ag_rsem,
):
    n = lax.axis_size("ctx")
    me, core = lax.axis_index("ctx"), lax.axis_index("dp")
    side = lax.rem(me, 2)
    rows, channels = up.shape
    half = channels // 2
    filt_rows = taps_here.shape[0]
    chunks, planes = data.shape[1], z_got.shape[1]
    size = rows + filt_rows
    packed = stage.shape[2]
    level = me // PLANE
    partner = {"dp": 1 - core}
    across = {"ctx": me + 1 - 2 * side}
    beside = {"ctx": me + 2 - 4 * (lax.rem(me, PLANE) // 2)}
    before, after = {"ctx": lax.rem(me + n - 2, n)}, {"ctx": lax.rem(me + 2, n)}
    has_before, has_after = me >= 2, me < n - 2

    def column(k):
        return {"ctx": lax.rem(me + k * PLANE, n)}

    def plane_at(k):
        return lax.rem(level + k, planes)

    barrier = pltpu.get_barrier_semaphore()
    peers = [partner, across, before, after] + [column(k) for k in range(1, planes)]
    for peer in peers:
        pl.semaphore_signal(barrier, inc=1, device_id=peer, device_id_type=MESH)

    def local(src, dst, sem):
        return pltpu.make_async_copy(src, dst, sem)

    def remote(src, dst, send, got, device):
        return pltpu.make_async_remote_copy(
            src_ref=src, dst_ref=dst, send_sem=send, recv_sem=got,
            device_id=device, device_id_type=MESH,
        )

    def source(g, owner, c, p):
        low = (owner * chunks + c) * LANES + p * half + max(g - 1, 0) * channels
        at = pl.ds(pl.multiple_of(low, LANES), LANES)
        return x.at[:, at] if g else up.at[:, at]

    def place(owner, c, g, p):
        return data.at[owner, c, g, :, pl.ds(p * LANES, LANES)]

    def own_start(c):
        for g in range(4):
            for p in range(2):
                local(source(g, side, c, p), place(side, c, g, p), own_sem.at[c]).start()

    def own_wait(c):
        local(data.at[1 - side, c], data.at[side, c], own_sem.at[c]).wait()

    def x_start(c):
        for g in range(4):
            for p in range(2):
                remote(
                    source(g, 1 - side, c, p), place(side, c, g, p),
                    x_ssem.at[c, g // 2], x_rsem.at[c, g // 2], across,
                ).start()

    def x_whole(c, part):
        block = data.at[1 - side, c, pl.ds(2 * part, 2)]
        return remote(block, block, x_ssem.at[c, part], x_rsem.at[c, part], across)

    def nxt_copy(c):
        return remote(
            data.at[0, c, pl.ds(0, 2)], data.at[2, c, pl.ds(0, 2)], nxt_ssem.at[c], nxt_rsem.at[c], before
        )

    def tail_copy(c):
        return remote(
            data.at[1, c, pl.ds(1, 3), pl.ds(rows - TAIL, TAIL)], prev.at[c],
            tail_ssem.at[c], tail_rsem.at[c], after,
        )

    def dp_copy(c):
        return remote(
            stage.at[c, 1 - core], dp_got.at[c], dp_ssem.at[c], dp_rsem.at[c], partner
        )

    def z_copy(c, k):
        return remote(
            z_part.at[c, plane_at(k)], z_got.at[c, level], z_ssem.at[c, k],
            z_rsem.at[c, level], column(k),
        )

    def z_arrival(c, k):
        return remote(
            z_part.at[c, 0], z_got.at[c, plane_at(k)], z_ssem.at[c, k],
            z_rsem.at[c, plane_at(k)], column(k),
        )

    def y_copy(c):
        return remote(y_part.at[c], y_got.at[c], y_ssem.at[c], y_rsem.at[c], beside)

    def e_copy(c):
        return remote(done.at[c], e_got.at[c], e_ssem.at[c], e_rsem.at[c], across)

    def ag_copy(c, foreign, k):
        owner = (side + foreign - 2 * side * foreign) * chunks + c
        return remote(
            (e_got if foreign else done).at[c], out.at[owner, level],
            ag_ssem.at[c, foreign, k], ag_rsem.at[owner, level], column(k),
        )

    def ag_arrival(owner, k):
        return remote(
            done.at[0], out.at[owner, plane_at(k)], ag_ssem.at[0, 0, k],
            ag_rsem.at[owner, plane_at(k)], column(k),
        )

    def out_copy(c, foreign):
        owner = (side + foreign - 2 * side * foreign) * chunks + c
        return local(
            (e_got if foreign else done).at[c], out.at[owner, level], out_sem.at[c, foreign]
        )

    taps_side = pl.ds(pl.multiple_of(side * chunks * LANES, LANES), chunks * LANES)
    swaps = (
        remote(taps_here.at[:, taps_side], taps_all.at[core], swap_ssem.at[0], swap_rsem.at[0], partner),
        remote(w_here, w_all.at[core], swap_ssem.at[1], swap_rsem.at[1], partner),
    )
    kept = [
        local(taps_here.at[:, taps_side], taps_all.at[core], fixed_sem.at[0]),
        local(w_here, w_all.at[core], fixed_sem.at[1]),
    ] + [local(f, m, fixed_sem.at[2 + i]) for i, (f, m) in enumerate(((f0, m0), (f1, m1), (f2, m2), (f3, m3)))]

    own_start(0)
    for copy in kept:
        copy.start()

    @pl.loop(1, chunks)
    def _(c):
        own_start(c)

    pl.semaphore_wait(barrier, len(peers))

    @pl.loop(0, AHEAD)
    def _(c):
        x_start(c)

    for copy in swaps:
        copy.start()

    @pl.when(me < 2)
    def _():
        prev[...] = jnp.zeros_like(prev)

    @pl.when(me >= n - 2)
    def _():
        data[2, :, 0:2] = jnp.zeros_like(data[2, :, 0:2])

    for copy in kept:
        copy.wait()
    own_wait(0)

    @pl.when((side == 0) & has_before)
    def _():
        nxt_copy(0).start()

    @pl.when((side == 1) & has_after)
    def _():
        tail_copy(0).start()

    for copy in swaps:
        copy.wait()

    def block_terms(c, b, t_hat, weights):
        def start(old):
            for g, ext in enumerate((q_ext, k_ext, v_ext)):
                ext[0:PAD, :] = old[g].astype(F32)[TAIL - PAD :]

        @pl.when(b == 0)
        def _():
            start(prev[c])

        @pl.when(b == 1)
        def _():
            start(data[0, c, 1:4, rows - TAIL :, :])

        for g, ext in enumerate((q_ext, k_ext, v_ext)):
            ext[PAD : PAD + rows, :] = data[b, c, g + 1].astype(F32)
        q_ext[PAD + rows : PAD + size, :] = data[b + 1, c, 1].astype(F32)
        up_ext[0:rows, :] = data[b, c, 0]
        up_ext[rows:size, :] = data[b + 1, c, 0]
        return chunk_terms(
            q_ext, k_ext, v_ext, up_ext, t_hat, weights, (m0, m2, m3), rows, reach
        )

    def compute(c):
        @pl.when(c + AHEAD < chunks)
        def _():
            x_start(c + AHEAD)

        @pl.when(c + 1 < chunks)
        def _():
            own_wait(c + 1)

        @pl.when((side == 0) & has_before & (c + 1 < chunks))
        def _():
            nxt_copy(c + 1).start()

        @pl.when((side == 1) & has_after & (c + 1 < chunks))
        def _():
            tail_copy(c + 1).start()

        x_whole(c, 0).wait_recv()

        @pl.when((side == 1) & has_before)
        def _():
            nxt_copy(c).start()

        x_whole(c, 1).wait_recv()

        @pl.when((side == 0) & has_after)
        def _():
            tail_copy(c).start()

        @pl.when((side == 0) & has_after)
        def _():
            nxt_copy(c).wait_recv()

        @pl.when((side == 1) & has_before)
        def _():
            tail_copy(c).wait_recv()

        here = pl.ds(pl.multiple_of(c * LANES, LANES), LANES)
        taps = jnp.concatenate([taps_all[p, :, here] for p in range(2)], 1)

        def weight(g, p):
            part, slot = divmod(2 * g + p, 3)
            low = (side * chunks + c) * LANES + slot * half
            return w_all[part, :, pl.ds(pl.multiple_of(low, LANES), LANES)]

        weights = [jnp.concatenate([weight(g, p) for p in range(2)], 1) for g in range(3)]
        t_hat = taps_transform(taps, m1)
        first = block_terms(c, 1 - side, t_hat, weights)

        @pl.when((side == 0) & has_before)
        def _():
            tail_copy(c).wait_recv()

        @pl.when((side == 1) & has_after)
        def _():
            nxt_copy(c).wait_recv()

        second = block_terms(c, side, t_hat, weights)
        cross_re, cross_im, feat_q, feat_k, feat_v = [a + b for a, b in zip(first, second)]
        filt = inverse(cross_re, cross_im, m3, filt_rows)
        a, b = slice(0, LANES), slice(LANES, 2 * LANES)
        rest = [jnp.zeros((packed - filt_rows - 3 * PAD, LANES), F32)]
        stage[c, 0] = jnp.concatenate(
            [filt[:, a], feat_q[:, a], feat_q[:, b], feat_k[:, a]] + rest, 0
        )
        stage[c, 1] = jnp.concatenate(
            [filt[:, b], feat_k[:, b], feat_v[:, a], feat_v[:, b]] + rest, 0
        )
        dp_copy(c).start()

    def along_z(c):
        dp_copy(c).wait_recv()
        pair = stage[c, core] + dp_got[c]
        z_part[c] = pair.reshape(planes, packed // planes, LANES).astype(BF16)
        for k in range(1, planes):
            z_copy(c, k).start()

    def along_y(c):
        cut = packed // planes
        mine = pl.ds(pl.multiple_of(level * cut, PAD), cut)
        total = stage[c, core, mine] + dp_got[c, mine]
        for k in range(1, planes):
            z_arrival(c, k).wait_recv()
            total += z_got[c, plane_at(k)].astype(F32)
        y_part[c] = total
        y_copy(c).start()

    def share(c, foreign):
        for k in range(1, planes):
            ag_copy(c, foreign, k).start()
        out_copy(c, foreign).start()

    def along_x(c):
        y_copy(c).wait_recv()
        done[c] = (y_part[c] + y_got[c]).astype(BF16)
        e_copy(c).start()
        share(c, 0)

    def finish(c):
        e_copy(c).wait_recv()
        share(c, 1)

    steps = ((compute, 0), (along_z, 1), (along_y, 2), (along_x, 3), (finish, 5))

    @pl.loop(0, chunks + steps[-1][1])
    def _(i):
        for step, lag in steps:
            @pl.when((i >= lag) & (i - lag < chunks))
            def _():
                step(i - lag)

    @pl.loop(0, chunks)
    def _(c):
        for k in range(1, planes):
            ag_arrival(c, k).wait_recv()
            ag_arrival(c + chunks, k).wait_recv()
        for foreign in range(2):
            out_copy(c, foreign).wait()
            for k in range(1, planes):
                ag_copy(c, foreign, k).wait_send()
        for part in range(2):
            x_whole(c, part).wait_send()
        dp_copy(c).wait_send()
        for k in range(1, planes):
            z_copy(c, k).wait_send()
        y_copy(c).wait_send()
        e_copy(c).wait_send()

    @pl.when(has_before)
    def _():
        @pl.loop(0, chunks)
        def _(c):
            nxt_copy(c).wait_send()

    @pl.when(has_after)
    def _():
        @pl.loop(0, chunks)
        def _(c):
            tail_copy(c).wait_send()


def unpack_kernel(scale, reach, got, filt, feat):
    filt_rows = filt.shape[0]
    half = got.shape[0] * LANES
    for owner in range(got.shape[0]):
        value = got[owner].astype(F32).reshape(-1, LANES) * scale
        filt[:, owner * LANES : (owner + 1) * LANES] = value[:filt_rows]
        for g in range(3):
            low = filt_rows + g * PAD
            at = owner * LANES + g * half
            feat[:, at : at + LANES] = value[low : low + reach]


def fused(inputs, feat_weight, filter_taps, upstream):
    x, up = inputs[0], upstream[0]
    n = lax.axis_size("ctx")
    rows, channels = up.shape
    filt_rows, reach = filter_taps.shape[0], feat_weight.shape[0]
    scale = (lax.axis_size("dp") * n * rows) ** (-0.5)
    mats = [jnp.asarray(m) for m in transforms(rows, filt_rows)]
    size = rows + filt_rows
    width = 2 * LANES
    chunks = channels // (2 * width)
    planes = n // PLANE
    packed = -(-(filt_rows + 3 * PAD) // (planes * PAD)) * (planes * PAD)
    cut = packed // planes
    dma = lambda *shape: pltpu.SemaphoreType.DMA(shape)
    anywhere = pl.BlockSpec(memory_space=pl.ANY)
    gathered = pl.pallas_call(
        functools.partial(fused_kernel, reach),
        out_shape=jax.ShapeDtypeStruct((2 * chunks, planes, cut, LANES), BF16),
        in_specs=[anywhere] * 8,
        out_specs=anywhere,
        scratch_shapes=[
            pltpu.VMEM((3, chunks, 4, rows, width), BF16),
            pltpu.VMEM((chunks, 3, TAIL, width), BF16),
            pltpu.VMEM((2, filt_rows, chunks * LANES), F32),
            pltpu.VMEM((2,) + feat_weight.shape, F32),
            *[pltpu.VMEM(m.shape, BF16) for m in mats],
            pltpu.VMEM((PAD + size, width), F32),
            pltpu.VMEM((PAD + rows, width), F32),
            pltpu.VMEM((PAD + rows, width), F32),
            pltpu.VMEM((size, width), BF16),
            pltpu.VMEM((chunks, 2, packed, LANES), F32),
            pltpu.VMEM((chunks, packed, LANES), F32),
            pltpu.VMEM((chunks, planes, cut, LANES), BF16),
            pltpu.VMEM((chunks, planes, cut, LANES), BF16),
            pltpu.VMEM((chunks, cut, LANES), F32),
            pltpu.VMEM((chunks, cut, LANES), F32),
            pltpu.VMEM((chunks, cut, LANES), BF16),
            pltpu.VMEM((chunks, cut, LANES), BF16),
            dma(chunks), dma(6), dma(chunks, 2), dma(2), dma(2),
            dma(chunks, 2), dma(chunks, 2),
            *[dma(chunks)] * 6,
            dma(chunks, planes), dma(chunks, planes),
            *[dma(chunks)] * 4,
            dma(chunks, 2, planes), dma(2 * chunks, planes),
        ],
        compiler_params=pltpu.CompilerParams(
            collective_id=0, has_side_effects=True, vmem_limit_bytes=63 * 2**20
        ),
    )(x, up, filter_taps, feat_weight, *mats)
    return pl.pallas_call(
        functools.partial(unpack_kernel, scale, reach),
        out_shape=[
            jax.ShapeDtypeStruct(filter_taps.shape, F32),
            jax.ShapeDtypeStruct(feat_weight.shape, F32),
        ],
        in_specs=[pl.BlockSpec(memory_space=pltpu.VMEM)],
        out_specs=[pl.BlockSpec(memory_space=pltpu.VMEM)] * 2,
    )(gathered)


def per_device(inputs, feat_weight, filter_taps, upstream):
    n = lax.axis_size("ctx")
    rows, channels = upstream.shape[1:]
    whole = n % PLANE == 0 and n // PLANE > 1 and channels == 2 * n * LANES
    square = rows == filter_taps.shape[0] and feat_weight.shape[0] <= PAD
    if lax.axis_size("dp") == 2 and whole and square and rows % TAIL == 0:
        return fused(inputs, feat_weight, filter_taps, upstream)
    return by_collectives(inputs, feat_weight, filter_taps, upstream)


def solution(mesh):
    placed = (P("dp", "ctx", None), P(None, "dp"), P(None, "dp"), P("dp", "ctx", None))
    return jax.shard_map(
        per_device,
        mesh=mesh,
        in_specs=placed,
        out_specs=(P(None, "dp"), P(None, "dp")),
        check_vma=False,
    )
```

```python
import functools

import jax
import jax.numpy as jnp
import numpy as np
from jax import lax
from jax.experimental import pallas as pl
from jax.experimental.pallas import tpu as pltpu
from jax.sharding import PartitionSpec as P

PAD = 8
F32 = jnp.float32
BF16 = jnp.bfloat16


def from_behind(block, axis, distance):
    devices = range(lax.axis_size(axis))
    route = [(i - distance, i) for i in devices if i - distance in devices]
    return lax.ppermute(block, axis, route)


def two_parts(matrix):
    high = matrix.astype(BF16)
    low = (matrix - high.astype(np.float64)).astype(BF16)
    return high, low


def transforms(rows, taps):
    size = rows + taps
    half = size // 2
    angle = 2 * np.pi * np.outer(np.arange(half), np.arange(size)) / size
    cosines = np.cos(angle)
    sines = -np.sin(angle)
    sines[0] = np.cos(np.pi * np.arange(size))
    forward = np.concatenate([cosines, sines], 0)
    weight = np.full((size, 1), 2.0 / size)
    weight[0] = weight[half] = 1.0 / size
    backward = (forward * weight).T
    f_high, f_low = two_parts(forward)
    b_high, b_low = two_parts(backward)
    cat = lambda *parts: np.concatenate(parts, 1)
    return (
        cat(f_high[:, :rows], f_low[:, :rows]),
        cat(f_high[:, :taps], f_low[:, :taps], f_high[:, :taps]),
        cat(f_high, f_low),
        cat(b_high, b_low),
    )


def dot(a, b):
    return jnp.dot(a, b, preferred_element_type=F32)


def taps_transform(taps, to_taps):
    taps_high = taps.astype(BF16)
    taps_low = (taps - taps_high.astype(F32)).astype(BF16)
    return dot(to_taps[...], jnp.concatenate([taps_high, taps_high, taps_low], 0))


def inverse(re, im, back, out_rows):
    re, im = re.astype(BF16), im.astype(BF16)
    return dot(back[:out_rows, :], jnp.concatenate([re, im, re, im], 0))


def chunk_terms(q_ext, k_ext, v_ext, up_ext, t_hat, weights, mats, rows, reach):
    to_mixed, to_grad, back = mats
    size = up_ext.shape[0]
    half = size // 2

    def featured(ext, w, out_rows):
        total = w[0:1] * ext[PAD : PAD + out_rows, :]
        for j in range(1, reach):
            total += w[j : j + 1] * ext[PAD - j : PAD - j + out_rows, :]
        return total

    def lagged(grad, ext, out_rows):
        sums = [
            jnp.sum(grad * ext[PAD - j : PAD - j + out_rows, :], 0, keepdims=True)
            for j in range(reach)
        ]
        sums += [jnp.zeros_like(sums[0])] * (PAD - reach)
        return jnp.concatenate(sums, 0)

    key_part = featured(k_ext, weights[1], rows)
    value_part = featured(v_ext, weights[2], rows)
    mixed = (key_part * value_part).astype(BF16)
    m_hat = dot(to_mixed[...], jnp.concatenate([mixed, mixed], 0))
    query = featured(q_ext, weights[0], size)
    grad_conv = (up_ext[...].astype(F32) * query).astype(BF16)
    g_hat = dot(to_grad[...], jnp.concatenate([grad_conv, grad_conv], 0))

    m_re, m_im = m_hat[:half], m_hat[half:]
    t_re, t_im = t_hat[:half], t_hat[half:]
    g_re, g_im = g_hat[:half], g_hat[half:]
    first = lax.broadcasted_iota(jnp.int32, m_re.shape, 0) == 0
    t_imz = jnp.where(first, 0.0, t_im)
    t_ren = jnp.where(first, t_im, t_re)
    m_imz = jnp.where(first, 0.0, m_im)
    m_ren = jnp.where(first, m_im, m_re)

    conv_out = inverse(
        m_re * t_re - m_im * t_imz, m_re * t_imz + m_im * t_ren, back, size
    )
    grad_mixed = inverse(
        g_re * t_re + g_im * t_imz, g_im * t_ren - g_re * t_imz, back, rows
    )
    return (
        g_re * m_re + g_im * m_imz,
        g_im * m_ren - g_re * m_imz,
        lagged(up_ext[...].astype(F32) * conv_out, q_ext, size),
        lagged(grad_mixed * value_part, k_ext, rows),
        lagged(grad_mixed * key_part, v_ext, rows),
    )


def local_kernel(
    reach, xq, xk, xv, pq, pk, pv, nq, up, nup, taps, wq, wk, wv, m0, m1, m2, m3,
    filt, fq, fk, fv, q_ext, k_ext, v_ext, up_ext,
):
    rows = xq.shape[0]
    size = up_ext.shape[0]
    for ext, prev, block in ((q_ext, pq, xq), (k_ext, pk, xk), (v_ext, pv, xv)):
        ext[0:PAD, :] = prev[...].astype(F32)
        ext[PAD : PAD + rows, :] = block[...].astype(F32)
    q_ext[PAD + rows : PAD + size, :] = nq[...].astype(F32)
    up_ext[0:rows, :] = up[...]
    up_ext[rows:size, :] = nup[...]
    t_hat = taps_transform(taps[...], m1)
    cross_re, cross_im, fq[...], fk[...], fv[...] = chunk_terms(
        q_ext, k_ext, v_ext, up_ext, t_hat, (wq[...], wk[...], wv[...]),
        (m0, m2, m3), rows, reach,
    )
    filt[...] = inverse(cross_re, cross_im, m3, taps.shape[0])


def by_collectives(inputs, feat_weight, filter_taps, upstream):
    inputs_here = inputs[0]
    grad_here = upstream[0]
    rows = inputs_here.shape[0]
    channels = grad_here.shape[1]
    filt_rows = filter_taps.shape[0]
    reach = feat_weight.shape[0]
    scale = (lax.axis_size("dp") * lax.axis_size("ctx") * rows) ** (-0.5)
    feat_full, taps_full = (
        lax.all_gather(feat_weight, "dp", axis=1, tiled=True),
        lax.all_gather(filter_taps, "dp", axis=1, tiled=True),
    )
    next_grad, next_query = from_behind(
        (grad_here[:filt_rows], inputs_here[:filt_rows, :channels]), "ctx", -1
    )
    before = from_behind(inputs_here[rows - PAD :], "ctx", 1)
    weights = jnp.concatenate(
        [feat_full, jnp.zeros((PAD - reach, feat_full.shape[1]), F32)], 0
    )
    mats = [jnp.asarray(m) for m in transforms(rows, filt_rows)]
    width = 256
    steps = channels // width
    size = rows + filt_rows
    part = lambda r, group: pl.BlockSpec((r, width), lambda i: (0, i + group * steps))
    whole = lambda m: pl.BlockSpec(m.shape, lambda i: (0, 0))
    out = lambda r: jax.ShapeDtypeStruct((r, channels), F32)
    filter_part, feat_q, feat_k, feat_v = pl.pallas_call(
        functools.partial(local_kernel, reach),
        grid=(steps,),
        out_shape=[out(filt_rows), out(PAD), out(PAD), out(PAD)],
        in_specs=[part(rows, g) for g in range(3)]
        + [part(PAD, g) for g in range(3)]
        + [part(filt_rows, 0), part(rows, 0), part(filt_rows, 0), part(filt_rows, 0)]
        + [part(PAD, g) for g in range(3)]
        + [whole(m) for m in mats],
        out_specs=[part(filt_rows, 0)] + [part(PAD, 0)] * 3,
        scratch_shapes=[
            pltpu.VMEM((PAD + size, width), F32),
            pltpu.VMEM((PAD + rows, width), F32),
            pltpu.VMEM((PAD + rows, width), F32),
            pltpu.VMEM((size, width), BF16),
        ],
    )(
        inputs_here, inputs_here, inputs_here, before, before, before, next_query,
        grad_here, next_grad, taps_full, weights, weights, weights, *mats,
    )
    feat_part = jnp.concatenate([feat_q, feat_k, feat_v], 1)[:reach]
    filter_summed, feat_summed = (
        lax.psum_scatter(filter_part, "dp", scatter_dimension=1, tiled=True),
        lax.psum_scatter(feat_part, "dp", scatter_dimension=1, tiled=True),
    )
    filter_whole, feat_whole = lax.psum((filter_summed, feat_summed), "ctx")
    return (filter_whole * scale, feat_whole * scale)


MESH = pl.DeviceIdType.MESH
LANES = 128
PLANE = 4
TAIL = 16
AHEAD = 2
LATE = 3


def fused_kernel(
    reach, x, up, taps_here, w_here, f0, f1, f2, f3, out,
    data, prev, taps_all, w_all, m0, m1, m2, m3, q_ext, k_ext, v_ext, up_ext,
    stage, dp_got, z_part, z_got, y_part, y_got, done, e_got,
    own_sem, fixed_sem, out_sem, swap_ssem, swap_rsem, x_ssem, x_rsem,
    nxt_ssem, nxt_rsem, tail_ssem, tail_rsem, dp_ssem, dp_rsem, z_ssem, z_rsem,
    y_ssem, y_rsem, e_ssem, e_rsem, ag_ssem, ag_rsem,
):
    n = lax.axis_size("ctx")
    me, core = lax.axis_index("ctx"), lax.axis_index("dp")
    side = lax.rem(me, 2)
    rows, channels = up.shape
    half = channels // 2
    filt_rows = taps_here.shape[0]
    chunks, planes = data.shape[1], z_got.shape[1]
    size = rows + filt_rows
    packed = stage.shape[2]
    level = me // PLANE
    partner = {"dp": 1 - core}
    across = {"ctx": me + 1 - 2 * side}
    beside = {"ctx": me + 2 - 4 * (lax.rem(me, PLANE) // 2)}
    before, after = {"ctx": lax.rem(me + n - 2, n)}, {"ctx": lax.rem(me + 2, n)}
    has_before, has_after = me >= 2, me < n - 2

    def column(k):
        return {"ctx": lax.rem(me + k * PLANE, n)}

    def plane_at(k):
        return lax.rem(level + k, planes)

    def over(k):
        return {"ctx": lax.rem(me + 1 - 2 * side + n + k * PLANE, n)}

    early = chunks - LATE
    barrier = pltpu.get_barrier_semaphore()
    peers = [partner, across, before, after]
    peers += [far(k) for k in range(1, planes) for far in (column, over)]
    for peer in peers:
        pl.semaphore_signal(barrier, inc=1, device_id=peer, device_id_type=MESH)

    def local(src, dst, sem):
        return pltpu.make_async_copy(src, dst, sem)

    def remote(src, dst, send, got, device):
        return pltpu.make_async_remote_copy(
            src_ref=src, dst_ref=dst, send_sem=send, recv_sem=got,
            device_id=device, device_id_type=MESH,
        )

    def source(g, owner, c, p):
        low = (owner * chunks + c) * LANES + p * half + max(g - 1, 0) * channels
        at = pl.ds(pl.multiple_of(low, LANES), LANES)
        return x.at[:, at] if g else up.at[:, at]

    def place(owner, c, g, p):
        return data.at[owner, c, g, :, pl.ds(p * LANES, LANES)]

    def own_start(c):
        for g in range(4):
            for p in range(2):
                local(source(g, side, c, p), place(side, c, g, p), own_sem.at[c]).start()

    def own_wait(c):
        local(data.at[1 - side, c], data.at[side, c], own_sem.at[c]).wait()

    def x_start(c, part):
        for g in range(2 * part, 2 * part + 2):
            for p in range(2):
                remote(
                    source(g, 1 - side, c, p), place(side, c, g, p),
                    x_ssem.at[c, part], x_rsem.at[c, part], across,
                ).start()

    def x_whole(c, part):
        block = data.at[1 - side, c, pl.ds(2 * part, 2)]
        return remote(block, block, x_ssem.at[c, part], x_rsem.at[c, part], across)

    def nxt_copy(c):
        return remote(
            data.at[0, c, pl.ds(0, 2)], data.at[2, c, pl.ds(0, 2)], nxt_ssem.at[c], nxt_rsem.at[c], before
        )

    def tail_copy(c):
        return remote(
            data.at[1, c, pl.ds(1, 3), pl.ds(rows - TAIL, TAIL)], prev.at[c],
            tail_ssem.at[c], tail_rsem.at[c], after,
        )

    def dp_copy(c):
        return remote(
            stage.at[c, 1 - core], dp_got.at[c], dp_ssem.at[c], dp_rsem.at[c], partner
        )

    def z_copy(c, k):
        return remote(
            z_part.at[c, plane_at(k)], z_got.at[c, level], z_ssem.at[c, k],
            z_rsem.at[c, level], column(k),
        )

    def z_arrival(c, k):
        return remote(
            z_part.at[c, 0], z_got.at[c, plane_at(k)], z_ssem.at[c, k],
            z_rsem.at[c, plane_at(k)], column(k),
        )

    def y_copy(c):
        return remote(y_part.at[c], y_got.at[c], y_ssem.at[c], y_rsem.at[c], beside)

    def e_copy(c):
        return remote(done.at[c], e_got.at[c], e_ssem.at[c], e_rsem.at[c], across)

    def ag_copy(c, foreign, k):
        owner = (side + foreign - 2 * side * foreign) * chunks + c
        return remote(
            (e_got if foreign else done).at[c], out.at[owner, level],
            ag_ssem.at[c, foreign, k], ag_rsem.at[owner, level], column(k),
        )

    def ag_arrival(owner, k):
        return remote(
            done.at[0], out.at[owner, plane_at(k)], ag_ssem.at[0, 0, k],
            ag_rsem.at[owner, plane_at(k)], across,
        )

    def over_copy(c, k):
        owner = side * chunks + c
        return remote(
            done.at[c], out.at[owner, level], ag_ssem.at[c, 1, k], ag_rsem.at[owner, level],
            over(k),
        )

    def out_copy(c, foreign):
        owner = (side + foreign - 2 * side * foreign) * chunks + c
        return local(
            (e_got if foreign else done).at[c], out.at[owner, level], out_sem.at[c, foreign]
        )

    taps_side = pl.ds(pl.multiple_of(side * chunks * LANES, LANES), chunks * LANES)
    swaps = (
        remote(taps_here.at[:, taps_side], taps_all.at[core], swap_ssem.at[0], swap_rsem.at[0], partner),
        remote(w_here, w_all.at[core], swap_ssem.at[1], swap_rsem.at[1], partner),
    )
    kept = [
        local(taps_here.at[:, taps_side], taps_all.at[core], fixed_sem.at[0]),
        local(w_here, w_all.at[core], fixed_sem.at[1]),
    ] + [local(f, m, fixed_sem.at[2 + i]) for i, (f, m) in enumerate(((f0, m0), (f1, m1), (f2, m2), (f3, m3)))]

    own_start(0)
    for copy in kept:
        copy.start()

    @pl.loop(1, chunks)
    def _(c):
        own_start(c)

    pl.semaphore_wait(barrier, len(peers))

    x_start(0, 0)

    @pl.loop(0, AHEAD)
    def _(c):
        x_start(c + 1, 0)
        x_start(c, 1)

    for copy in swaps:
        copy.start()

    @pl.when(me < 2)
    def _():
        prev[...] = jnp.zeros_like(prev)

    @pl.when(me >= n - 2)
    def _():
        data[2, :, 0:2] = jnp.zeros_like(data[2, :, 0:2])

    for copy in kept:
        copy.wait()
    own_wait(0)

    @pl.when((side == 0) & has_before)
    def _():
        nxt_copy(0).start()

    @pl.when((side == 1) & has_after)
    def _():
        tail_copy(0).start()

    for copy in swaps:
        copy.wait()

    x_whole(0, 0).wait_recv()

    @pl.when((side == 1) & has_before)
    def _():
        nxt_copy(0).start()

    def block_terms(c, b, t_hat, weights):
        def start(old):
            for g, ext in enumerate((q_ext, k_ext, v_ext)):
                ext[0:PAD, :] = old[g].astype(F32)[TAIL - PAD :]

        @pl.when(b == 0)
        def _():
            start(prev[c])

        @pl.when(b == 1)
        def _():
            start(data[0, c, 1:4, rows - TAIL :, :])

        for g, ext in enumerate((q_ext, k_ext, v_ext)):
            ext[PAD : PAD + rows, :] = data[b, c, g + 1].astype(F32)
        q_ext[PAD + rows : PAD + size, :] = data[b + 1, c, 1].astype(F32)
        up_ext[0:rows, :] = data[b, c, 0]
        up_ext[rows:size, :] = data[b + 1, c, 0]
        return chunk_terms(
            q_ext, k_ext, v_ext, up_ext, t_hat, weights, (m0, m2, m3), rows, reach
        )

    def compute(c):
        @pl.when(c + AHEAD + 1 < chunks)
        def _():
            x_start(c + AHEAD + 1, 0)

        @pl.when(c + AHEAD < chunks)
        def _():
            x_start(c + AHEAD, 1)

        @pl.when(c + 1 < chunks)
        def _():
            own_wait(c + 1)

        @pl.when((side == 0) & has_before & (c + 1 < chunks))
        def _():
            nxt_copy(c + 1).start()

        @pl.when((side == 1) & has_after & (c + 1 < chunks))
        def _():
            tail_copy(c + 1).start()

        @pl.when(c + 1 < chunks)
        def _():
            x_whole(c + 1, 0).wait_recv()

        @pl.when((side == 1) & has_before & (c + 1 < chunks))
        def _():
            nxt_copy(c + 1).start()

        x_whole(c, 1).wait_recv()

        @pl.when((side == 0) & has_after)
        def _():
            tail_copy(c).start()

        @pl.when((side == 0) & has_after)
        def _():
            nxt_copy(c).wait_recv()

        @pl.when((side == 1) & has_before)
        def _():
            tail_copy(c).wait_recv()

        here = pl.ds(pl.multiple_of(c * LANES, LANES), LANES)
        taps = jnp.concatenate([taps_all[p, :, here] for p in range(2)], 1)

        def weight(g, p):
            part, slot = divmod(2 * g + p, 3)
            low = (side * chunks + c) * LANES + slot * half
            return w_all[part, :, pl.ds(pl.multiple_of(low, LANES), LANES)]

        weights = [jnp.concatenate([weight(g, p) for p in range(2)], 1) for g in range(3)]
        t_hat = taps_transform(taps, m1)
        first = block_terms(c, 1 - side, t_hat, weights)

        @pl.when((side == 0) & has_before)
        def _():
            tail_copy(c).wait_recv()

        @pl.when((side == 1) & has_after)
        def _():
            nxt_copy(c).wait_recv()

        second = block_terms(c, side, t_hat, weights)
        cross_re, cross_im, feat_q, feat_k, feat_v = [a + b for a, b in zip(first, second)]
        filt = inverse(cross_re, cross_im, m3, filt_rows)
        a, b = slice(0, LANES), slice(LANES, 2 * LANES)
        rest = [jnp.zeros((packed - filt_rows - 3 * PAD, LANES), F32)]
        stage[c, 0] = jnp.concatenate(
            [filt[:, a], feat_q[:, a], feat_q[:, b], feat_k[:, a]] + rest, 0
        )
        stage[c, 1] = jnp.concatenate(
            [filt[:, b], feat_k[:, b], feat_v[:, a], feat_v[:, b]] + rest, 0
        )
        dp_copy(c).start()

    def along_z(c):
        dp_copy(c).wait_recv()
        pair = stage[c, core] + dp_got[c]
        z_part[c] = pair.reshape(planes, packed // planes, LANES).astype(BF16)
        for k in range(1, planes):
            z_copy(c, k).start()

    def along_y(c):
        cut = packed // planes
        mine = pl.ds(pl.multiple_of(level * cut, PAD), cut)
        total = stage[c, core, mine] + dp_got[c, mine]
        for k in range(1, planes):
            z_arrival(c, k).wait_recv()
            total += z_got[c, plane_at(k)].astype(F32)
        y_part[c] = total
        y_copy(c).start()

    def share(c, foreign):
        for k in range(1, planes):
            ag_copy(c, foreign, k).start()
        out_copy(c, foreign).start()

    def along_x(c):
        y_copy(c).wait_recv()
        done[c] = (y_part[c] + y_got[c]).astype(BF16)
        @pl.when(c < early)
        def _():
            e_copy(c).start()

        @pl.when(c >= early)
        def _():
            for k in range(planes):
                over_copy(c, k).start()

        share(c, 0)

    def finish(c):
        @pl.when(c < early)
        def _():
            e_copy(c).wait_recv()
            share(c, 1)

    steps = ((compute, 0), (along_z, 1), (along_y, 2), (along_x, 3), (finish, 5))

    @pl.loop(0, chunks + steps[-1][1])
    def _(i):
        for step, lag in steps:
            @pl.when((i >= lag) & (i - lag < chunks))
            def _():
                step(i - lag)

    @pl.loop(0, chunks)
    def _(c):
        for k in range(1, planes):
            ag_arrival(c, k).wait_recv()
            ag_arrival(c + chunks, k).wait_recv()
        out_copy(c, 0).wait()
        for k in range(1, planes):
            ag_copy(c, 0, k).wait_send()

        @pl.when(c < early)
        def _():
            e_copy(c).wait_send()
            out_copy(c, 1).wait()
            for k in range(1, planes):
                ag_copy(c, 1, k).wait_send()

        @pl.when(c >= early)
        def _():
            ag_arrival((1 - side) * chunks + c, 0).wait_recv()
            for k in range(planes):
                over_copy(c, k).wait_send()

        for part in range(2):
            x_whole(c, part).wait_send()
        dp_copy(c).wait_send()
        for k in range(1, planes):
            z_copy(c, k).wait_send()
        y_copy(c).wait_send()

    @pl.when(has_before)
    def _():
        @pl.loop(0, chunks)
        def _(c):
            nxt_copy(c).wait_send()

    @pl.when(has_after)
    def _():
        @pl.loop(0, chunks)
        def _(c):
            tail_copy(c).wait_send()


def unpack_kernel(scale, reach, got, filt, feat):
    filt_rows = filt.shape[0]
    half = got.shape[0] * LANES
    for owner in range(got.shape[0]):
        value = got[owner].astype(F32).reshape(-1, LANES) * scale
        filt[:, owner * LANES : (owner + 1) * LANES] = value[:filt_rows]
        for g in range(3):
            low = filt_rows + g * PAD
            at = owner * LANES + g * half
            feat[:, at : at + LANES] = value[low : low + reach]


def fused(inputs, feat_weight, filter_taps, upstream):
    x, up = inputs[0], upstream[0]
    n = lax.axis_size("ctx")
    rows, channels = up.shape
    filt_rows, reach = filter_taps.shape[0], feat_weight.shape[0]
    scale = (lax.axis_size("dp") * n * rows) ** (-0.5)
    mats = [jnp.asarray(m) for m in transforms(rows, filt_rows)]
    size = rows + filt_rows
    width = 2 * LANES
    chunks = channels // (2 * width)
    planes = n // PLANE
    packed = -(-(filt_rows + 3 * PAD) // (planes * PAD)) * (planes * PAD)
    cut = packed // planes
    dma = lambda *shape: pltpu.SemaphoreType.DMA(shape)
    anywhere = pl.BlockSpec(memory_space=pl.ANY)
    gathered = pl.pallas_call(
        functools.partial(fused_kernel, reach),
        out_shape=jax.ShapeDtypeStruct((2 * chunks, planes, cut, LANES), BF16),
        in_specs=[anywhere] * 8,
        out_specs=anywhere,
        scratch_shapes=[
            pltpu.VMEM((3, chunks, 4, rows, width), BF16),
            pltpu.VMEM((chunks, 3, TAIL, width), BF16),
            pltpu.VMEM((2, filt_rows, chunks * LANES), F32),
            pltpu.VMEM((2,) + feat_weight.shape, F32),
            *[pltpu.VMEM(m.shape, BF16) for m in mats],
            pltpu.VMEM((PAD + size, width), F32),
            pltpu.VMEM((PAD + rows, width), F32),
            pltpu.VMEM((PAD + rows, width), F32),
            pltpu.VMEM((size, width), BF16),
            pltpu.VMEM((chunks, 2, packed, LANES), F32),
            pltpu.VMEM((chunks, packed, LANES), F32),
            pltpu.VMEM((chunks, planes, cut, LANES), BF16),
            pltpu.VMEM((chunks, planes, cut, LANES), BF16),
            pltpu.VMEM((chunks, cut, LANES), F32),
            pltpu.VMEM((chunks, cut, LANES), F32),
            pltpu.VMEM((chunks, cut, LANES), BF16),
            pltpu.VMEM((chunks, cut, LANES), BF16),
            dma(chunks), dma(6), dma(chunks, 2), dma(2), dma(2),
            dma(chunks, 2), dma(chunks, 2),
            *[dma(chunks)] * 6,
            dma(chunks, planes), dma(chunks, planes),
            *[dma(chunks)] * 4,
            dma(chunks, 2, planes), dma(2 * chunks, planes),
        ],
        compiler_params=pltpu.CompilerParams(
            collective_id=0, has_side_effects=True, vmem_limit_bytes=63 * 2**20
        ),
    )(x, up, filter_taps, feat_weight, *mats)
    return pl.pallas_call(
        functools.partial(unpack_kernel, scale, reach),
        out_shape=[
            jax.ShapeDtypeStruct(filter_taps.shape, F32),
            jax.ShapeDtypeStruct(feat_weight.shape, F32),
        ],
        in_specs=[pl.BlockSpec(memory_space=pltpu.VMEM)],
        out_specs=[pl.BlockSpec(memory_space=pltpu.VMEM)] * 2,
    )(gathered)


def per_device(inputs, feat_weight, filter_taps, upstream):
    n = lax.axis_size("ctx")
    rows, channels = upstream.shape[1:]
    whole = n % PLANE == 0 and n // PLANE > 1 and channels == 2 * n * LANES
    square = rows == filter_taps.shape[0] and feat_weight.shape[0] <= PAD
    if lax.axis_size("dp") == 2 and whole and square and rows % TAIL == 0:
        return fused(inputs, feat_weight, filter_taps, upstream)
    return by_collectives(inputs, feat_weight, filter_taps, upstream)


def solution(mesh):
    placed = (P("dp", "ctx", None), P(None, "dp"), P(None, "dp"), P("dp", "ctx", None))
    return jax.shard_map(
        per_device,
        mesh=mesh,
        in_specs=placed,
        out_specs=(P(None, "dp"), P(None, "dp")),
        check_vma=False,
    )
```
